32 devices in a mesh: dp: 8 (over y, x, core), tensor: 4 (over z).
Axes of the slice: x: 2, y: 2, z: 4, core: 2. Of those that a mesh axis runs over, the one named last changes fastest.
Arguments:
- layer_input: bfloat16 [2048, 8, 768], P('tensor', 'dp'), may hold values from -6 to 6
- segments: int32 [8, 2048], P('dp'), may hold values from 0 to 64, as said below
- qkv_weight: bfloat16 [768, 2304], P(None, 'tensor'), may hold values from -0.21875 to 0.21875
- out_weight: bfloat16 [768, 768], P('tensor'), may hold values from -1.25 to 1.25
- gate_weight: bfloat16 [768, 3072], P(None, 'tensor'), may hold values from -0.21875 to 0.21875
- up_weight: bfloat16 [768, 3072], P(None, 'tensor'), may hold values from -0.21875 to 0.21875
- down_weight: bfloat16 [3072, 768], P('tensor'), may hold values from -0.109375 to 0.109375
- norm_params: float32 [4, 768], replicated, may hold values from -1.2 to 1.5, as said below
- cotangent: bfloat16 [2048, 8, 768], P('tensor', 'dp'), may hold values from -6 to 6
Outputs:
- layer_output: bfloat16 [2048, 8, 768], P('tensor', 'dp')
- input_grad: float32 [2048, 8, 768], P('tensor', 'dp')
- qkv_grad: float32 [768, 2304], P(None, 'tensor')
- out_grad: float32 [768, 768], P('tensor')
- gate_grad: float32 [768, 3072], P(None, 'tensor')
- up_grad: float32 [768, 3072], P(None, 'tensor')
- down_grad: float32 [3072, 768], P('tensor')
- norm_grads: float32 [4, 768], replicated
The draws below stay inside these ranges and needn't reach their ends.
Inputs may be any that keep to these rules, and one draw needn't show every extreme that they name: `segments`: in each row, segment numbers never fall and each document's positions are contiguous; every document of a row has 20 or more positions; positions after the row's last document hold 64 (padding). Some row is one document of 2048 tokens, some row ends in padding. `norm_params`: rows 0 and 2 are gains, rows 1 and 3 are biases.
All inputs are finite; a program needn't handle non-finite values.
Results may differ from the reference program's by a relative error of at most 0.023.
Values may be sent and summed in bfloat16 or wider, within the bound.
No kernel may reach another device: no remote copies, remote signals or barrier semaphores. Data moves between devices by JAX's collectives and lax.ppermute only.
A program may use at most 128 MiB of HBM per device.

```python
import jax
import jax.numpy as jnp
from jax import lax

D = 768
HEADS = 12
HEAD_DIM = 64
FF = 3072
ROW_LEN = 2048
MINDOC = 20
MAXDOCS = 64
ROWS = 8


def row_layout(key):
    base = jax.random.fold_in(key, 11)
    level_key, size_key = jax.random.split(base)
    row_ids = jnp.arange(ROWS, dtype=jnp.int32)
    level = jax.random.randint(level_key, (ROWS,), 0, 4, dtype=jnp.int32)
    level = jnp.where(row_ids % 8 == 0, 0, level)
    level = jnp.where(row_ids % 8 == 1, 1, level)
    limit = jnp.maximum(jnp.right_shift(jnp.full((ROWS,), ROW_LEN, jnp.int32), 2 * level), MINDOC)
    raw = jax.random.randint(size_key, (ROWS, MAXDOCS), 0, 1 << 30, dtype=jnp.int32)
    sizes = MINDOC + raw % (limit[:, None] - MINDOC + 1)
    slot_ids = jnp.arange(MAXDOCS, dtype=jnp.int32)
    whole = (row_ids[:, None] % 8 == 0) & (slot_ids[None, :] == 0)
    sizes = jnp.where(whole, ROW_LEN, sizes)
    room = ROW_LEN - (row_ids % 8 == 1).astype(jnp.int32)
    ends = jnp.cumsum(sizes, axis=1, dtype=jnp.int32)
    lengths = jnp.where(ends <= room[:, None], sizes, 0).astype(jnp.int32)
    kept_ends = jnp.cumsum(lengths, axis=1, dtype=jnp.int32)
    places = jnp.arange(ROW_LEN, dtype=jnp.int32)
    segments = jnp.sum(kept_ends[:, None, :] <= places[None, :, None], axis=2, dtype=jnp.int32)
    return segments


def draw_segments(key, part):
    return row_layout(key)


def draw_norm_params(key, part):
    gain_key, bias_key = jax.random.split(jax.random.fold_in(key, 5))
    gains = 1.0 + 0.5 * jax.random.uniform(gain_key, (2, D), jnp.float32, -1.0, 1.0)
    biases = jnp.clip(0.3 * jax.random.normal(bias_key, (2, D), jnp.float32), -1.2, 1.2)
    return jnp.stack([gains[0], biases[0], gains[1], biases[1]], axis=0)


def levels(rng, extent, shards, least, largest):
    level = 1.0
    for axis_at, blocks in shards:
        steps = jax.random.uniform(jax.random.fold_in(jax.random.fold_in(rng, 6), axis_at), (blocks,), jnp.float32, least / len(shards), largest / len(shards))
        level = level * jnp.repeat(jnp.exp(steps), extent[axis_at] // blocks).reshape((-1,) + (1,) * (len(extent) - 1 - axis_at))
    return level


def scatter_about(rng, dims, width, most, pieces=(), held_as=jnp.bfloat16):
    level = levels(rng, dims, pieces, -0.22, 0.18) if pieces else 1.0
    array = jax.random.normal(rng, dims, jnp.float32) * width * level
    return jnp.minimum(jnp.maximum(array, -most), most).astype(held_as)


def setup_inputs(seed: int = 0) -> dict:
    splits = jax.random.split(jax.random.key(seed), 10)
    return {
        "layer_input": scatter_about(splits[0], (ROW_LEN, ROWS, D), 1.0, 6.0, ((0, 4), (1, 8))),
        "segments": draw_segments(jax.random.fold_in(splits[9], 71), 0),
        "qkv_weight": scatter_about(splits[2], (D, 3 * HEADS * HEAD_DIM), D ** -0.5, 0.21875, ((1, 4),)),
        "out_weight": scatter_about(splits[3], (HEADS * HEAD_DIM, D), (HEADS * HEAD_DIM // 32) ** -0.5, 1.25, ((0, 4),)),
        "gate_weight": scatter_about(splits[4], (D, FF), D ** -0.5, 0.21875, ((1, 4),)),
        "up_weight": scatter_about(splits[5], (D, FF), D ** -0.5, 0.21875, ((1, 4),)),
        "down_weight": scatter_about(splits[6], (FF, D), FF ** -0.5, 0.109375, ((0, 4),)),
        "norm_params": draw_norm_params(jax.random.fold_in(splits[9], 71), 0),
        "cotangent": scatter_about(splits[8], (ROW_LEN, ROWS, D), 1.0, 6.0, ((0, 4), (1, 8))),
    }


EPSILON = 1e-05
ROPE_BASE = 1000.0
NEGATIVE = -1e+30
HIGHEST = lax.Precision.HIGHEST

@jax.custom_vjp
def low(v):
    return lax.optimization_barrier(v.astype(jnp.bfloat16)).astype(jnp.float32)

@jax.custom_vjp
def low_back(v):
    return v

def low_keep(v):
    return (low(v), None)

def low_pass(kept, grad):
    return (grad,)

def back_keep(v):
    return (v, None)

def back_low(kept, grad):
    return (low(grad),)
low.defvjp(low_keep, low_pass)
low_back.defvjp(back_keep, back_low)

def layer_norm(total, gain, bias):
    center = lax.optimization_barrier(jnp.mean(total, axis=-1, keepdims=True))
    shifted = total - center
    spread = lax.optimization_barrier(jnp.mean(shifted * shifted, axis=-1, keepdims=True))
    return shifted * lax.rsqrt(spread + EPSILON) * gain + bias

def positions_of(segment_row):
    labels = jnp.arange(MAXDOCS + 1, dtype=jnp.int32)
    chosen = segment_row[:, None] == labels[None, :]
    counts = lax.optimization_barrier(jnp.sum(chosen.astype(jnp.int32), axis=0, dtype=jnp.int32))
    starts = jnp.cumsum(counts, dtype=jnp.int32) - counts
    first = lax.optimization_barrier(jnp.sum(jnp.where(chosen, starts[None, :], 0), axis=1, dtype=jnp.int32))
    return jnp.arange(segment_row.shape[0], dtype=jnp.int32) - first

def rotary_tables(positions, depth):
    half = depth // 2
    powers = jnp.arange(half, dtype=jnp.float32) * (-2.0 / depth)
    inverse = ROPE_BASE ** powers
    angles = positions.astype(jnp.float32)[..., None] * inverse
    return (jnp.cos(angles), jnp.sin(angles))

def rotate(field, cosine, sine):
    half = field.shape[-1] // 2
    first = field[..., :half]
    second = field[..., half:]
    return jnp.concatenate([first * cosine - second * sine, second * cosine + first * sine], axis=-1)

def layer_row(params, row_input, segment_row):
    qkv_weight, out_weight, gate_weight, up_weight, down_weight, norm_params = params
    length = row_input.shape[0]
    scale = HEAD_DIM ** (-0.5)
    joint = low_back(jnp.dot(row_input, qkv_weight, precision=HIGHEST)).reshape(length, HEADS, 3, HEAD_DIM)
    cosine, sine = rotary_tables(positions_of(segment_row), HEAD_DIM)
    cosine = cosine[:, None, :]
    sine = sine[:, None, :]
    queries = low(rotate(joint[:, :, 0], cosine, sine))
    keys = low(rotate(joint[:, :, 1], cosine, sine))
    values = low(joint[:, :, 2])
    block = min(512, length)
    places = jnp.arange(length, dtype=jnp.int32)

    def one_block(start):
        query_block = lax.dynamic_slice_in_dim(queries, start, block, 0)
        segment_block = lax.dynamic_slice_in_dim(segment_row, start, block, 0)
        block_places = start + jnp.arange(block, dtype=jnp.int32)
        scores = low_back(jnp.einsum('qhd,khd->hqk', query_block, keys, precision=HIGHEST) * scale)
        same = segment_block[:, None] == segment_row[None, :]
        live = (segment_block[:, None] < MAXDOCS) | (block_places[:, None] == places[None, :])
        scores = jnp.where((same & live)[None], scores, NEGATIVE)
        highest = lax.optimization_barrier(jnp.max(scores, axis=-1, keepdims=True))
        expo = jnp.exp(scores - highest)
        probs = low(expo / lax.optimization_barrier(jnp.sum(expo, axis=-1, keepdims=True)))
        return jnp.einsum('hqk,khd->qhd', probs, values, precision=HIGHEST)
    starts = jnp.arange(length // block, dtype=jnp.int32) * block
    mixed = lax.map(jax.checkpoint(one_block), starts).reshape(length, HEADS * HEAD_DIM)
    mixed = low_back(low(mixed))
    attention = low_back(jnp.dot(mixed, out_weight, precision=HIGHEST))
    normed = layer_norm(row_input + attention, norm_params[0], norm_params[1])
    normed_low = low(normed)
    gate = low_back(jnp.dot(normed_low, gate_weight, precision=HIGHEST))
    up = low_back(jnp.dot(normed_low, up_weight, precision=HIGHEST))
    hidden = low(jax.nn.silu(gate) * up)
    branch = low_back(jnp.dot(hidden, down_weight, precision=HIGHEST))
    return layer_norm(normed + branch, norm_params[2], norm_params[3])

def reference(layer_input, segments, qkv_weight, out_weight, gate_weight, up_weight, down_weight, norm_params, cotangent):
    weights = tuple((matrix.astype(jnp.float32) for matrix in (qkv_weight, out_weight, gate_weight, up_weight, down_weight)))
    params = weights + (norm_params.astype(jnp.float32),)
    inputs = jnp.transpose(layer_input.astype(jnp.float32), (1, 0, 2))
    row_layer = jax.checkpoint(layer_row)

    def forward(inputs, params):

        def step(carry, row):
            return (carry, row_layer(params, row[0], row[1]))
        unused, outputs = lax.scan(step, jnp.zeros((), jnp.float32), (inputs, segments))
        return outputs
    outputs, pull = jax.vjp(forward, inputs, params)
    input_grad, param_grads = pull(jnp.transpose(cotangent.astype(jnp.float32), (1, 0, 2)))
    return (jnp.transpose(outputs, (1, 0, 2)).astype(jnp.bfloat16), jnp.transpose(input_grad, (1, 0, 2)), param_grads[0], param_grads[1], param_grads[2], param_grads[3], param_grads[4], param_grads[5])
```

```python
import functools

import jax
import jax.numpy as jnp
from jax import lax
from jax.experimental import pallas as pl
from jax.experimental.pallas import tpu as pltpu
from jax.sharding import PartitionSpec as P

HEAD_DIM = 64
MAXDOCS = 64
EPSILON = 1e-05
ROPE_BASE = 1000.0
NEGATIVE = -1e30
LOG2E = 1.4426950408889634
BF = jnp.bfloat16
F32 = jnp.float32


def dotg(a, b, ca, cb):
    return lax.dot_general(a, b, (((ca,), (cb,)), ((), ())), preferred_element_type=F32)


def forward_kernel(
    heads, hd, T, nt, nat_ref, kind_ref, x_ref, wt_ref, cos_ref, sin_ref, segq_ref, segk_ref,
    jt_ref, ot_ref, lse_ref, knat,
):
    half = hd // 2
    for b in range(nt):
        cols = slice(b * T, (b + 1) * T)
        jt = dotg(wt_ref[...], x_ref[b], 1, 1)
        c = cos_ref[:, cols]
        s = sin_ref[:, cols]
        for h in range(heads):
            base = 3 * hd * h
            for w in range(2):
                lo = jt[base + w * hd : base + w * hd + half]
                hi = jt[base + w * hd + half : base + (w + 1) * hd]
                turned = jnp.concatenate([lo * c - hi * s, hi * c + lo * s], axis=0).astype(BF)
                if w == 0:
                    turned = turned * jnp.asarray(hd**-0.5, BF)
                else:
                    knat[h, cols, :] = turned.T
                jt_ref[base + w * hd : base + (w + 1) * hd, cols] = turned
            jt_ref[base + 2 * hd : base + 3 * hd, cols] = jt[base + 2 * hd : base + 3 * hd].astype(BF)

    def query_step(qi, _):
        qs = pl.ds(pl.multiple_of(qi * T, T), T)
        segq = segq_ref[0:1, qs]

        def tile(kj, carry, masked):
            ks = pl.ds(pl.multiple_of(kj * T, T), T)
            out = []
            if masked:
                ok = segk_ref[ks, 0:1] == segq
            for h in range(heads):
                top, total, acc = carry[h]
                base = 3 * hd * h
                q = jt_ref[base : base + hd, qs]
                v = jt_ref[base + 2 * hd : base + 3 * hd, ks]
                s = dotg(knat[h, ks, :], q, 1, 0)
                if masked:
                    s = jnp.where(ok, s, NEGATIVE)
                new = jnp.maximum(top, jnp.max(s, axis=0, keepdims=True))
                p = jnp.exp2(s * LOG2E - new * LOG2E)
                if masked:
                    p = jnp.where(ok, p, 0.0)
                keep = jnp.exp2((top - new) * LOG2E)
                total = total * keep + jnp.sum(p, axis=0, keepdims=True)
                acc = acc * keep + dotg(v, p.astype(BF), 1, 0)
                out.append((new, total, acc))
            return tuple(out)

        def body(kj, carry):
            return lax.switch(
                kind_ref[qi, kj],
                [lambda c: c, lambda c: tile(kj, c, False), lambda c: tile(kj, c, True)],
                carry,
            )

        start = tuple(
            (jnp.full((1, T), NEGATIVE, F32), jnp.zeros((1, T), F32), jnp.zeros((hd, T), F32))
            for _ in range(heads)
        )
        done = lax.fori_loop(0, nt, body, start)
        for h in range(heads):
            top, total, acc = done[h]
            ot_ref[nat_ref[qi], h * hd : (h + 1) * hd, :] = (acc / total).astype(BF)
            lse_ref[h : h + 1, qs] = top * LOG2E + jnp.log2(total)
        return 0

    lax.fori_loop(0, nt, query_step, 0)


def backward_kernel(
    heads, hd, T, nt, nat_ref, kind_ref, jt_ref, ot_ref, gt_ref, lse_ref, cos_ref, sin_ref,
    segq_ref, segk_ref, jg_ref, knat, vnat, qnat, gnat, dk, dv, dl,
):
    half = hd // 2
    scale = hd**-0.5
    for h in range(heads):
        base = 3 * hd * h
        rows = slice(h * hd, (h + 1) * hd)
        for b in range(nt):
            cols = slice(b * T, (b + 1) * T)
            qnat[h, cols, :] = jt_ref[base : base + hd, cols].T
            knat[h, cols, :] = jt_ref[base + hd : base + 2 * hd, cols].T
            vnat[h, cols, :] = jt_ref[base + 2 * hd : base + 3 * hd, cols].T
            g = gt_ref[nat_ref[b], rows, :]
            gnat[h, cols, :] = g.T
            o = ot_ref[nat_ref[b], rows, :]
            dl[h : h + 1, cols] = jnp.sum(g.astype(F32) * o.astype(F32), axis=0, keepdims=True)
    dk[...] = jnp.zeros_like(dk)
    dv[...] = jnp.zeros_like(dv)

    def unturn(grad, cols):
        c = cos_ref[:, cols]
        s = sin_ref[:, cols]
        lo, hi = grad[:half], grad[half:]
        return jnp.concatenate([lo * c + hi * s, hi * c - lo * s], axis=0).astype(BF)

    def query_step(qi, _):
        qs = pl.ds(pl.multiple_of(qi * T, T), T)
        segq = segq_ref[0:1, qs]

        def tile(kj, carry, masked):
            ks = pl.ds(pl.multiple_of(kj * T, T), T)
            out = []
            if masked:
                ok = segk_ref[ks, 0:1] == segq
            for h in range(heads):
                base = 3 * hd * h
                s = dotg(knat[h, ks, :], jt_ref[base : base + hd, qs], 1, 0)
                if masked:
                    s = jnp.where(ok, s, NEGATIVE)
                p = jnp.exp2(s * LOG2E - lse_ref[h : h + 1, qs])
                dp = dotg(vnat[h, ks, :], gt_ref[nat_ref[qi], h * hd : (h + 1) * hd, :], 1, 0)
                ds = (p * (dp - dl[h : h + 1, qs])).astype(BF)
                dv[h, ks, :] += dotg(p.astype(BF), gnat[h, qs, :], 1, 0)
                dk[h, ks, :] += dotg(ds, qnat[h, qs, :], 1, 0)
                out.append(carry[h] + dotg(jt_ref[base + hd : base + 2 * hd, ks], ds, 1, 0))
            return tuple(out)

        def body(kj, carry):
            return lax.switch(
                kind_ref[qi, kj],
                [lambda c: c, lambda c: tile(kj, c, False), lambda c: tile(kj, c, True)],
                carry,
            )

        done = lax.fori_loop(0, nt, body, tuple(jnp.zeros((hd, T), F32) for _ in range(heads)))
        for h in range(heads):
            jg_ref[3 * hd * h : 3 * hd * h + hd, qs] = unturn(done[h] * scale, qs)
        return 0

    lax.fori_loop(0, nt, query_step, 0)
    for h in range(heads):
        base = 3 * hd * h
        for b in range(nt):
            cols = slice(b * T, (b + 1) * T)
            jg_ref[base + hd : base + 2 * hd, cols] = unturn(dk[h, cols, :].T, cols)
            jg_ref[base + 2 * hd : base + 3 * hd, cols] = dv[h, cols, :].T.astype(BF)


VM = pl.BlockSpec(memory_space=pltpu.VMEM)
SM = pl.BlockSpec(memory_space=pltpu.SMEM)
VMEM_BYTES = 60 * 1024 * 1024


def attend_forward(nat, kind, x, wt, cosine, sine, segq, segk):
    nt, T, _ = x.shape
    cols = wt.shape[0] // 3
    heads = cols // HEAD_DIM
    length = nt * T
    return pl.pallas_call(
        functools.partial(forward_kernel, heads, HEAD_DIM, T, nt),
        out_shape=(
            jax.ShapeDtypeStruct((3 * cols, length), BF),
            jax.ShapeDtypeStruct((nt, cols, T), BF),
            jax.ShapeDtypeStruct((heads, length), F32),
        ),
        in_specs=[SM] * 2 + [VM] * 6,
        out_specs=[VM] * 3,
        scratch_shapes=[pltpu.VMEM((heads, length, HEAD_DIM), BF)],
        cost_estimate=pl.CostEstimate(
            flops=16 * heads * length * length * HEAD_DIM,
            bytes_accessed=12_000_000,
            transcendentals=heads * length * length,
        ),
        compiler_params=pltpu.CompilerParams(vmem_limit_bytes=VMEM_BYTES),
        name="attend_forward",
    )(nat, kind, x, wt, cosine, sine, segq, segk)


def attend_backward(nat, kind, jt, ot, gt, lse, cosine, sine, segq, segk):
    nt, cols, T = ot.shape
    heads = cols // HEAD_DIM
    length = nt * T
    return pl.pallas_call(
        functools.partial(backward_kernel, heads, HEAD_DIM, T, nt),
        out_shape=jax.ShapeDtypeStruct((3 * cols, length), BF),
        in_specs=[SM] * 2 + [VM] * 8,
        out_specs=VM,
        scratch_shapes=[pltpu.VMEM((heads, length, HEAD_DIM), BF)] * 4
        + [pltpu.VMEM((heads, length, HEAD_DIM), F32)] * 2
        + [pltpu.VMEM((heads, length), F32)],
        cost_estimate=pl.CostEstimate(
            flops=40 * heads * length * length * HEAD_DIM,
            bytes_accessed=12_000_000,
            transcendentals=heads * length * length,
        ),
        compiler_params=pltpu.CompilerParams(vmem_limit_bytes=VMEM_BYTES),
        name="attend_backward",
    )(nat, kind, jt, ot, gt, lse, cosine, sine, segq, segk)


def positions_of(segment_row):
    labels = jnp.arange(MAXDOCS + 1, dtype=jnp.int32)
    chosen = segment_row[:, None] == labels[None, :]
    counts = jnp.sum(chosen.astype(jnp.int32), axis=0, dtype=jnp.int32)
    starts = jnp.cumsum(counts, dtype=jnp.int32) - counts
    first = jnp.sum(jnp.where(chosen, starts[None, :], 0), axis=1, dtype=jnp.int32)
    return jnp.arange(segment_row.shape[0], dtype=jnp.int32) - first


def norm_forward(total, gain, bias):
    center = jnp.mean(total, axis=-1, keepdims=True)
    shifted = total - center
    inverse = lax.rsqrt(jnp.mean(shifted * shifted, axis=-1, keepdims=True) + EPSILON)
    hat = shifted * inverse
    return hat * gain + bias, hat, inverse


def norm_backward(incoming, hat, inverse, gain):
    h = incoming * gain
    mean_h = jnp.mean(h, axis=-1, keepdims=True)
    mean_hz = jnp.mean(h * hat, axis=-1, keepdims=True)
    grad = inverse * (h - mean_h - hat * mean_hz)
    return grad, jnp.sum(incoming * hat, axis=0), jnp.sum(incoming, axis=0)


def butterfly_sum(value, sizes):
    for axis, size in sizes:
        step = 1
        while step < size:
            value = value + lax.ppermute(value, axis, [(i, i ^ step) for i in range(size)])
            step *= 2
    return value


def per_device(
    layer_input,
    segments,
    qkv_weight,
    out_weight,
    gate_weight,
    up_weight,
    down_weight,
    norm_params,
    cotangent,
):
    piece_len, _, width = layer_input.shape
    parts = lax.axis_size("tensor")
    rows_dp = lax.axis_size("dp")
    me = lax.axis_index("tensor")
    my_dp = lax.axis_index("dp")
    x = layer_input[:, 0]
    shard_ff = gate_weight.shape[1]
    head_cols = out_weight.shape[0]

    own = jnp.concatenate([gate_weight.T, up_weight.T, down_weight, out_weight], axis=0)
    own_rows = own.shape[0]
    slice_rows = own_rows // rows_dp
    sent = lax.dynamic_slice_in_dim(own, my_dp * slice_rows, slice_rows, 0)
    full = lax.all_gather(sent, ("tensor", "dp"), axis=0, tiled=True)
    full = full.reshape(parts, own_rows, width)

    middle = (me == 1) | (me == 2)
    pair = [(i, i ^ 1) for i in range(parts)]
    cross = [(1, 2), (2, 1)]
    outward = [(1, 0), (2, 3)]
    near = lax.ppermute(x, "tensor", pair)
    cross_own = lax.ppermute(x, "tensor", cross)
    cross_near = lax.ppermute(near, "tensor", cross)
    out_own = lax.ppermute(cross_own, "tensor", outward)
    out_near = lax.ppermute(cross_near, "tensor", outward)
    gathered = jnp.stack(
        [x, near, jnp.where(middle, cross_near, out_own), jnp.where(middle, cross_own, out_near)]
    )

    segment_row = segments[0]
    nat = me ^ jnp.arange(parts, dtype=jnp.int32)
    powers = jnp.arange(HEAD_DIM // 2, dtype=F32) * (-2.0 / HEAD_DIM)
    places = positions_of(segment_row).reshape(parts, piece_len)
    places = jnp.take(places, nat, axis=0).reshape(-1)
    angles = places.astype(F32)[None, :] * (ROPE_BASE**powers)[:, None]
    cosine, sine = jnp.cos(angles), jnp.sin(angles)
    marks = jnp.where(
        segment_row < MAXDOCS,
        segment_row,
        MAXDOCS + jnp.arange(segment_row.shape[0], dtype=jnp.int32),
    ).reshape(parts, piece_len)
    marks = jnp.take(marks, nat, axis=0)
    low, high = jnp.min(marks, axis=1), jnp.max(marks, axis=1)
    meet = (low[:, None] <= high[None, :]) & (low[None, :] <= high[:, None])
    same = (low == high)[:, None] & (low == high)[None, :] & (low[:, None] == low[None, :])
    kind = jnp.where(same, 1, jnp.where(meet, 2, 0)).astype(jnp.int32)
    segq = marks.reshape(1, -1)
    segk = marks.reshape(-1, 1)

    joint, heads_t, logsum = attend_forward(
        nat, kind, gathered, qkv_weight.T, cosine, sine, segq, segk
    )
    mixed = lax.all_to_all(heads_t, "tensor", 0, 0, tiled=True).reshape(parts * head_cols, piece_len)

    gate_w = full[:, :shard_ff]
    up_w = full[:, shard_ff : 2 * shard_ff]
    down_w = full[:, 2 * shard_ff : 3 * shard_ff]
    out_w = full[:, 3 * shard_ff :].reshape(parts * head_cols, width)

    attention = dotg(mixed, out_w, 0, 0)
    normed, hat_one, inverse_one = norm_forward(
        x.astype(F32) + attention, norm_params[0], norm_params[1]
    )
    normed_low = normed.astype(BF)
    gate = jnp.einsum("td,kfd->ktf", normed_low, gate_w, preferred_element_type=F32)
    up = jnp.einsum("td,kfd->ktf", normed_low, up_w, preferred_element_type=F32)
    sig = jax.nn.sigmoid(gate)
    hidden = (gate * sig * up).astype(BF)
    branch = jnp.einsum("ktf,kfd->td", hidden, down_w, preferred_element_type=F32)
    output, hat_two, inverse_two = norm_forward(normed + branch, norm_params[2], norm_params[3])
    second_grad, gain_two, bias_two = norm_backward(
        cotangent[:, 0].astype(F32), hat_two, inverse_two, norm_params[2]
    )
    branch_low = second_grad.astype(BF)
    hidden_grad = jnp.einsum("td,kfd->ktf", branch_low, down_w, preferred_element_type=F32)
    gate_low = (hidden_grad * up * sig * (1 + gate * (1 - sig))).astype(BF)
    up_low = (hidden_grad * gate * sig).astype(BF)
    down_part = jnp.einsum("ktf,td->kfd", hidden, branch_low, preferred_element_type=F32)
    gate_part = jnp.einsum("ktf,td->kfd", gate_low, normed_low, preferred_element_type=F32)
    up_part = jnp.einsum("ktf,td->kfd", up_low, normed_low, preferred_element_type=F32)
    normed_grad = (
        second_grad
        + jnp.einsum("ktf,kfd->td", gate_low, gate_w, preferred_element_type=F32)
        + jnp.einsum("ktf,kfd->td", up_low, up_w, preferred_element_type=F32)
    )
    first_grad, gain_one, bias_one = norm_backward(normed_grad, hat_one, inverse_one, norm_params[0])
    attention_low = first_grad.astype(BF)
    heads_grad = dotg(out_w, attention_low, 1, 1).astype(BF).reshape(parts, head_cols, piece_len)
    out_part = dotg(mixed, attention_low, 1, 0).reshape(parts, head_cols, width)
    grad_t = lax.all_to_all(heads_grad, "tensor", 0, 0, tiled=True)

    parts_all = jnp.concatenate(
        [gate_part.astype(BF), up_part.astype(BF), down_part.astype(BF), out_part.astype(BF)], axis=1
    )
    parts_all = parts_all.reshape(parts, rows_dp, slice_rows, width).transpose(1, 0, 2, 3)
    summed = lax.psum_scatter(parts_all, "dp", scatter_dimension=0, tiled=True)[0]
    summed = lax.psum_scatter(summed, "tensor", scatter_dimension=0, tiled=True)[0]
    shard = lax.all_gather(summed, "dp", axis=0, tiled=True).astype(F32)

    joint_grad = attend_backward(
        nat, kind, joint, heads_t, grad_t, logsum, cosine, sine, segq, segk
    )
    inputs_flat = gathered.reshape(parts * piece_len, width)
    qkv_part = dotg(joint_grad, inputs_flat, 1, 0).astype(BF)
    qkv_grad = lax.psum(qkv_part, "dp").astype(F32).T

    share = dotg(joint_grad, qkv_weight, 0, 1).reshape(parts, piece_len, width)
    inward = [(0, 1), (3, 2)]
    zero = jnp.zeros((), F32)
    got_far = lax.ppermute(share[3].astype(BF), "tensor", inward).astype(F32)
    got_next = lax.ppermute(share[2].astype(BF), "tensor", inward).astype(F32)
    far = lax.ppermute((share[2] + got_far).astype(BF), "tensor", cross).astype(F32)
    mine = lax.ppermute((share[3] + got_next).astype(BF), "tensor", cross).astype(F32)
    last = lax.ppermute((share[1] + jnp.where(middle, far, zero)).astype(BF), "tensor", pair)
    input_grad = first_grad + share[0] + last.astype(F32) + jnp.where(middle, mine, zero)

    norm_grads = butterfly_sum(
        jnp.stack([gain_one, bias_one, gain_two, bias_two], axis=0),
        (("dp", rows_dp), ("tensor", parts)),
    )
    return (
        output.astype(BF)[:, None],
        input_grad[:, None],
        qkv_grad,
        shard[3 * shard_ff :],
        shard[:shard_ff].T,
        shard[shard_ff : 2 * shard_ff].T,
        shard[2 * shard_ff : 3 * shard_ff],
        norm_grads,
    )


def solution(mesh):
    placed = (
        P("tensor", "dp", None),
        P("dp", None),
        P(None, "tensor"),
        P("tensor", None),
        P(None, "tensor"),
        P(None, "tensor"),
        P("tensor", None),
        P(),
        P("tensor", "dp", None),
    )
    return jax.shard_map(
        per_device,
        mesh=mesh,
        in_specs=placed,
        out_specs=(
            P("tensor", "dp", None),
            P("tensor", "dp", None),
            P(None, "tensor"),
            P("tensor", None),
            P(None, "tensor"),
            P(None, "tensor"),
            P("tensor", None),
            P(),
        ),
        check_vma=False,
    )
```
